32 devices in a mesh: vec: 8 (over z, y), pair: 4 (over x, core).
Axes of the slice: x: 2, y: 2, z: 4, core: 2. Of those that a mesh axis runs over, the one named last changes fastest.
Arguments:
- green: bfloat16 [256, 32768], P('vec', 'pair'), may hold values from -6 to 6
- chol: bfloat16 [24576, 32768], P('vec', 'pair'), may hold values from -0.03125 to 0.03125
- fields: bfloat16 [256, 24576], P(None, 'vec'), may hold values from -5 to 5
Outputs:
- potential: float32 [256, 32768], P('vec', 'pair')
- log_weight: float32 [256], P('pair')
The draws below stay inside these ranges and needn't reach their ends.
All inputs are finite; a program needn't handle non-finite values.
Results may differ from the reference program's by a relative error of at most 0.0026.
Values may be sent and summed in bfloat16 or wider, within the bound.
A program may use at most 128 MiB of HBM per device.

```python
import jax
import jax.numpy as jnp
from jax import lax

NCHOL = 24576
NPAIR = 32768
WALKERS = 256


def level_of(rng, extent, split, smallest, top_value):
    def one(axis_at, blocks):
        steps = jax.random.uniform(jax.random.fold_in(jax.random.fold_in(rng, 6), axis_at), (blocks,), jnp.float32, smallest / len(split), top_value / len(split))
        return jnp.repeat(jnp.exp(steps), extent[axis_at] // blocks).reshape((-1,) + (1,) * (len(extent) - axis_at - 1))

    level = one(*split[0])
    for cut in split[1:]:
        level = level * one(*cut)
    return level


def gaussian(rng, dims, spread, bound, shards=(), held_as=jnp.bfloat16):
    result = spread * jax.random.normal(rng, dims, jnp.float32)
    if shards:
        result = result * level_of(rng, dims, shards, -0.22, 0.18)
    return jnp.clip(result, -bound, bound).astype(held_as)


def setup_inputs(seed: int = 0) -> dict:
    splits = jax.random.split(jax.random.key(seed), 4)
    return {
        "green": gaussian(splits[0], (WALKERS, NPAIR), 1.0, 6.0, ((0, 8), (1, 4))),
        "chol": gaussian(splits[1], (NCHOL, NPAIR), NPAIR ** -0.5, 0.03125, ((0, 8), (1, 4))),
        "fields": gaussian(splits[2], (WALKERS, NCHOL), 1.0, 5.0, ((1, 8),)),
    }


def reference(green, chol, fields):
    force = lax.dot_general(green, chol, (((1,), (1,)), ((), ())), preferred_element_type=jnp.float32)
    bias = jnp.tanh(force)
    field_values = fields.astype(jnp.float32)
    shifted = (field_values - bias).astype(jnp.bfloat16)
    potential = jnp.dot(shifted, chol, preferred_element_type=jnp.float32)
    log_weight = jnp.sum(field_values * bias - 0.5 * bias * bias, axis=1) / NCHOL
    return potential, log_weight
```

```python
import functools

import jax
import jax.numpy as jnp
from jax import lax
from jax.experimental import pallas as pl
from jax.experimental.pallas import tpu as pltpu
from jax.sharding import PartitionSpec as P

MESH = pl.DeviceIdType.MESH
LAG = 4
BUFS = 3


def kernel(
    dims,
    green_ref, chol_ref, fields_ref, out_ref, lw_ref,
    G, F, r1, s2, r2, SH, fbuf, acc, cb1, cb2, tmp, yS, yR, keep, zS, zR, lw_in,
    c1_sem, c2_sem, f_sem,
    gz_s, gz_r, gy_s, gy_r, e1_s, e1_r, e2_s, e2_r, e3_s, e3_r, e4_s, e4_r,
    py_s, py_r, pz_s, pz_r, lw_s, lw_r,
):
    V, Z, NP, X, LW, S, C, K, NK, KB, NC, CB, NB, TN = dims
    W = V * LW
    v = lax.axis_index("vec")
    p = lax.axis_index("pair")
    z, y = v // 2, v % 2
    x, q = p // 2, p % 2
    y_peer = (z * 2 + 1 - y, p)
    core_peer = (v, x * 2 + 1 - q)

    def z_at(d):
        return lax.rem(z + d, Z)

    def x_at(d):
        return lax.rem(x + d, X)

    def remote(src, dst, send, recv, to):
        return pltpu.make_async_remote_copy(
            src_ref=src, dst_ref=dst, send_sem=send, recv_sem=recv, device_id=to, device_id_type=MESH
        )

    def chol1(i):
        k, c = i // NC, i % NC
        rows = pl.ds(pl.multiple_of(c * CB, CB), CB)
        cols = pl.ds(pl.multiple_of(k * KB, KB), KB)
        slot = i % BUFS
        return pltpu.make_async_copy(chol_ref.at[rows, cols], cb1.at[slot], c1_sem.at[slot])

    def chol2(b):
        cols = pl.ds(pl.multiple_of(b * TN, TN), TN)
        slot = b % 2
        return pltpu.make_async_copy(chol_ref.at[:, cols], cb2.at[slot], c2_sem.at[slot])

    for i in range(BUFS - 1):
        chol1(i).start()
    chol2(0).start()
    own_rows = pl.ds(pl.multiple_of(p * S, S), S)
    load_fields = pltpu.make_async_copy(fields_ref.at[own_rows, :], fbuf, f_sem)
    load_fields.start()
    for k in range(NK):
        G[k, v] = green_ref[:, k * KB:(k + 1) * KB]

    barrier = pltpu.get_barrier_semaphore()
    for d in range(1, V):
        pl.semaphore_signal(barrier, inc=1, device_id=(lax.rem(v + d, V), p), device_id_type=MESH)
    pl.semaphore_signal(barrier, inc=1, device_id=core_peer, device_id_type=MESH)
    for d in range(1, X):
        pl.semaphore_signal(barrier, inc=1, device_id=(v, x_at(d) * 2 + q), device_id_type=MESH)
    pl.semaphore_wait(barrier, V - 1 + X)

    def gather_z(k, d):
        return remote(G.at[k, v], G.at[k, v], gz_s.at[k, d - 1], gz_r.at[k, d - 1], (z_at(d) * 2 + y, p))

    def gather_z_in(k, d):
        at = G.at[k, z_at(Z - d) * 2 + y]
        return remote(at, at, gz_s.at[k, d - 1], gz_r.at[k, d - 1], y_peer)

    def gather_y(k, d):
        at = G.at[k, z_at(Z - d) * 2 + y]
        return remote(at, at, gy_s.at[k, d], gy_r.at[k, d], y_peer)

    def gather_y_in(k, d):
        at = G.at[k, z_at(Z - d) * 2 + 1 - y]
        return remote(at, at, gy_s.at[k, d], gy_r.at[k, d], y_peer)

    def start_gather(k, carry):
        for d in range(1, Z):
            gather_z(k, d).start()
        gather_y(k, 0).start()
        return carry

    lax.fori_loop(0, NK, start_gather, 0)
    F[...] = jnp.zeros_like(F)
    acc[...] = jnp.zeros_like(acc)

    def forward(k):
        for d in range(1, Z):
            gather_z_in(k, d).wait_recv()
            gather_y(k, d).start()

    forward(0)

    def reduce_core(c):
        return remote(F.at[c, 1 - q], r1.at[c], e1_s.at[c], e1_r.at[c], core_peer)

    def force_step(i, carry):
        k, c = i // NC, i % NC

        @pl.when(c == 0)
        def _():
            @pl.when(k < NK - 1)
            def _():
                forward(k + 1)

            for d in range(Z):
                gather_y_in(k, d).wait_recv()

        @pl.when(i + BUFS - 1 < NK * NC)
        def _():
            chol1(i + BUFS - 1).start()

        chol1(i).wait()
        part = lax.dot_general(
            G[k].reshape(W, KB), cb1[i % BUFS], (((1,), (1,)), ((), ())), preferred_element_type=jnp.float32
        ).reshape(X, 2, S, CB)
        for h in range(2):
            F[c, h] += part[:, h]

        @pl.when(k == NK - 1)
        def _():
            reduce_core(c).start()

        return carry

    lax.fori_loop(0, NK * NC, force_step, 0)
    load_fields.wait()

    def reduce_x(c, d):
        return remote(s2.at[c, d - 1], r2.at[c, d - 1], e2_s.at[c, d - 1], e2_r.at[c, d - 1], (v, x_at(d) * 2 + q))

    def sum_cores(c, carry):
        reduce_core(c).wait_recv()
        for d in range(1, X):
            s2[c, d - 1] = F[c, q, x_at(d)] + r1[c, x_at(d)]
            reduce_x(c, d).start()
        return carry

    lax.fori_loop(0, NC, sum_cores, 0)

    def share_x(c, d):
        at = SH.at[c, p]
        return remote(at, at, e3_s.at[c, d - 1], e3_r.at[c, d - 1], (v, x_at(d) * 2 + q))

    def share_x_in(c, d):
        at = SH.at[c, x_at(X - d) * 2 + q]
        return remote(at, at, e3_s.at[c, d - 1], e3_r.at[c, d - 1], core_peer)

    def share_core(c, d):
        at = SH.at[c, x_at(X - d) * 2 + q]
        return remote(at, at, e4_s.at[c, d], e4_r.at[c, d], core_peer)

    def share_core_in(c, d):
        at = SH.at[c, x_at(X - d) * 2 + 1 - q]
        return remote(at, at, e4_s.at[c, d], e4_r.at[c, d], core_peer)

    def shift(c, carry):
        total = F[c, q, x] + r1[c, x]
        for d in range(1, X):
            reduce_x(c, d).wait_recv()
            total += r2[c, d - 1]
        bias = jnp.tanh(total)
        field = fbuf[:, pl.ds(pl.multiple_of(c * CB, CB), CB)].astype(jnp.float32)
        SH[c, p] = (field - bias).astype(jnp.bfloat16)
        for d in range(1, X):
            share_x(c, d).start()
        share_core(c, 0).start()
        terms = field * bias - 0.5 * bias * bias
        add = terms[:, :128]
        for j in range(1, CB // 128):
            add += terms[:, j * 128:(j + 1) * 128]
        acc[:S, :] += add
        return carry

    lax.fori_loop(0, NC, shift, 0)

    lw_in[0] = lax.dot_general(
        jnp.ones((8, 128), jnp.float32), acc[...], (((1,), (1,)), ((), ())),
        precision=lax.Precision.HIGHEST, preferred_element_type=jnp.float32,
    )

    def share_weight(d):
        return remote(lw_in.at[0], lw_in.at[d], lw_s.at[d - 1], lw_r.at[d - 1], (lax.rem(v + d, V), p))

    for d in range(1, V):
        share_weight(d).start()

    def pass_core(c, carry):
        for d in range(1, X):
            share_x_in(c, d).wait_recv()
            share_core(c, d).start()
        return carry

    lax.fori_loop(0, NC, pass_core, 0)

    def take_core(c, carry):
        for d in range(X):
            share_core_in(c, d).wait_recv()
        return carry

    lax.fori_loop(0, NC, take_core, 0)

    def scatter_y(b):
        return remote(yS.at[b], yR.at[b], py_s.at[b], py_r.at[b], y_peer)

    def scatter_z(b, d):
        return remote(zS.at[b, d - 1], zR.at[b, d - 1], pz_s.at[b, d - 1], pz_r.at[b, d - 1], (z_at(d) * 2 + y, p))

    def potential_step(b, carry):
        @pl.when(b < NB)
        def _():
            @pl.when(b + 1 < NB)
            def _():
                chol2(b + 1).start()

            chol2(b).wait()
            slot = b % 2
            total = jnp.zeros((W, TN), jnp.float32)
            for c in range(NC):
                total += jnp.dot(
                    SH[c].reshape(W, CB), cb2[slot, c * CB:(c + 1) * CB, :], preferred_element_type=jnp.float32
                )
            tmp[...] = total.reshape(Z, 2, LW, TN)
            yS[b] = tmp[:, 1 - y].astype(jnp.bfloat16)
            scatter_y(b).start()
            keep[b] = tmp[:, y]

        @pl.when(b >= LAG)
        def _():
            e = b - LAG
            scatter_y(e).wait_recv()
            for d in range(1, Z):
                zS[e, d - 1] = (keep[e, z_at(d)] + yR[e, z_at(d)].astype(jnp.float32)).astype(jnp.bfloat16)
                scatter_z(e, d).start()

        return carry

    lax.fori_loop(0, NB + LAG, potential_step, 0)

    def finish(b, carry):
        total = keep[b, z] + yR[b, z].astype(jnp.float32)
        for d in range(1, Z):
            scatter_z(b, d).wait_recv()
            total += zR[b, d - 1].astype(jnp.float32)
        out_ref[:, pl.ds(pl.multiple_of(b * TN, TN), TN)] = total
        return carry

    lax.fori_loop(0, NB, finish, 0)

    weight = lw_in[0]
    for d in range(1, V):
        share_weight(d).wait_recv()
        weight += lw_in[d]
        share_weight(d).wait_send()
    lw_ref[...] = weight

    def sent_gather(k, carry):
        for d in range(1, Z):
            gather_z(k, d).wait_send()
        for d in range(Z):
            gather_y(k, d).wait_send()
        return carry

    lax.fori_loop(0, NK, sent_gather, 0)

    def sent_share(c, carry):
        reduce_core(c).wait_send()
        for d in range(1, X):
            reduce_x(c, d).wait_send()
            share_x(c, d).wait_send()
        for d in range(X):
            share_core(c, d).wait_send()
        return carry

    lax.fori_loop(0, NC, sent_share, 0)

    def sent_scatter(b, carry):
        scatter_y(b).wait_send()
        for d in range(1, Z):
            scatter_z(b, d).wait_send()
        return carry

    lax.fori_loop(0, NB, sent_scatter, 0)


def shards(green, chol, fields):
    V, NP = lax.axis_size("vec"), lax.axis_size("pair")
    Z, X = V // 2, NP // 2
    LW, K = green.shape
    C = chol.shape[0]
    W = V * LW
    S = W // NP
    NK = 8
    KB = K // NK
    CB = 512
    NC = C // CB
    TN = 512
    NB = K // TN
    dims = (V, Z, NP, X, LW, S, C, K, NK, KB, NC, CB, NB, TN)
    bf, f32 = jnp.bfloat16, jnp.float32
    dma = pltpu.SemaphoreType.DMA
    potential, weight = pl.pallas_call(
        functools.partial(kernel, dims),
        out_shape=(jax.ShapeDtypeStruct((LW, K), f32), jax.ShapeDtypeStruct((8, 128), f32)),
        in_specs=[
            pl.BlockSpec(memory_space=pltpu.VMEM),
            pl.BlockSpec(memory_space=pl.ANY),
            pl.BlockSpec(memory_space=pl.ANY),
        ],
        out_specs=(pl.BlockSpec(memory_space=pltpu.VMEM), pl.BlockSpec(memory_space=pltpu.VMEM)),
        scratch_shapes=[
            pltpu.VMEM((NK, V, LW, KB), bf),
            pltpu.VMEM((NC, 2, X, S, CB), f32),
            pltpu.VMEM((NC, X, S, CB), f32),
            pltpu.VMEM((NC, X - 1, S, CB), f32),
            pltpu.VMEM((NC, X - 1, S, CB), f32),
            pltpu.VMEM((NC, NP, S, CB), bf),
            pltpu.VMEM((S, C), bf),
            pltpu.VMEM((128, 128), f32),
            pltpu.VMEM((BUFS, CB, KB), bf),
            pltpu.VMEM((2, C, TN), bf),
            pltpu.VMEM((Z, 2, LW, TN), f32),
            pltpu.VMEM((NB, Z, LW, TN), bf),
            pltpu.VMEM((NB, Z, LW, TN), bf),
            pltpu.VMEM((NB, Z, LW, TN), f32),
            pltpu.VMEM((NB, Z - 1, LW, TN), bf),
            pltpu.VMEM((NB, Z - 1, LW, TN), bf),
            pltpu.VMEM((V, 8, 128), f32),
            dma((BUFS,)), dma((2,)), dma(()),
            dma((NK, Z - 1)), dma((NK, Z - 1)), dma((NK, Z)), dma((NK, Z)),
            dma((NC,)), dma((NC,)), dma((NC, X - 1)), dma((NC, X - 1)),
            dma((NC, X - 1)), dma((NC, X - 1)), dma((NC, X)), dma((NC, X)),
            dma((NB,)), dma((NB,)), dma((NB, Z - 1)), dma((NB, Z - 1)),
            dma((V - 1,)), dma((V - 1,)),
        ],
        compiler_params=pltpu.CompilerParams(
            collective_id=0, has_side_effects=True, vmem_limit_bytes=56 * 1024 * 1024
        ),
        name="walker_step",
    )(green, chol, fields)
    return potential, weight[0, :S] / (C * V)


def solution(mesh):
    return jax.shard_map(
        shards,
        mesh=mesh,
        in_specs=(P("vec", "pair"), P("vec", "pair"), P(None, "vec")),
        out_specs=(P("vec", "pair"), P("pair")),
        check_vma=False,
    )
```

```python
import functools

import jax
import jax.numpy as jnp
from jax import lax
from jax.experimental import pallas as pl
from jax.experimental.pallas import tpu as pltpu
from jax.sharding import PartitionSpec as P

MESH = pl.DeviceIdType.MESH
LAG = 4
BUFS = 4
AHEAD = 3


def kernel(
    dims,
    green_ref, chol_ref, fields_ref, out_ref, lw_ref,
    G, F, r1, s2, r2, SH, fbuf, acc, cb1, cb2, tmp, yS, yR, keep, zS, zR, lw_in,
    c1_sem, c2_sem, f_sem,
    gz_s, gz_r, gy_s, gy_r, e1_s, e1_r, e2_s, e2_r, e3_s, e3_r, e4_s, e4_r,
    py_s, py_r, pz_s, pz_r, lw_s, lw_r,
):
    V, Z, NP, X, LW, S, C, K, NK, KB, NC, CB, NB, TN = dims
    HL, W2, S2, VS = LW // 2, V * LW // 2, S // 2, S // LW
    v = lax.axis_index("vec")
    p = lax.axis_index("pair")
    z, y = v // 2, v % 2
    x, q = p // 2, p % 2
    y_peer = (z * 2 + 1 - y, p)
    core_peer = (v, x * 2 + 1 - q)

    def z_at(d):
        return lax.rem(z + d, Z)

    def x_at(d):
        return lax.rem(x + d, X)

    def remote(src, dst, send, recv, to):
        return pltpu.make_async_remote_copy(
            src_ref=src, dst_ref=dst, send_sem=send, recv_sem=recv, device_id=to, device_id_type=MESH
        )

    def chol1(i):
        k, c = i // NC % NK, i % NC
        rows = pl.ds(pl.multiple_of(c * CB, CB), CB)
        cols = pl.ds(pl.multiple_of(k * KB, KB), KB)
        slot = i % BUFS
        return pltpu.make_async_copy(chol_ref.at[rows, cols], cb1.at[slot], c1_sem.at[slot])

    def chol2(t):
        cols = pl.ds(pl.multiple_of(t % NB * TN, TN), TN)
        slot = t % 2
        return pltpu.make_async_copy(chol_ref.at[:, cols], cb2.at[slot], c2_sem.at[slot])

    for i in range(BUFS - 1):
        chol1(i).start()
    chol2(0).start()
    load_fields = pltpu.make_async_copy(fields_ref.at[pl.ds(p * VS, VS)], fbuf, f_sem)
    load_fields.start()
    for h in range(2):
        for k in range(NK):
            G[h * NK + k, v] = green_ref[h * HL:(h + 1) * HL, k * KB:(k + 1) * KB]

    barrier = pltpu.get_barrier_semaphore()
    for d in range(1, V):
        pl.semaphore_signal(barrier, inc=1, device_id=(lax.rem(v + d, V), p), device_id_type=MESH)
    pl.semaphore_signal(barrier, inc=1, device_id=core_peer, device_id_type=MESH)
    for d in range(1, X):
        pl.semaphore_signal(barrier, inc=1, device_id=(v, x_at(d) * 2 + q), device_id_type=MESH)
    pl.semaphore_wait(barrier, V - 1 + X)

    def gather_z(k, d):
        return remote(G.at[k, v], G.at[k, v], gz_s.at[k, d - 1], gz_r.at[k, d - 1], (z_at(d) * 2 + y, p))

    def gather_z_in(k, d):
        at = G.at[k, z_at(Z - d) * 2 + y]
        return remote(at, at, gz_s.at[k, d - 1], gz_r.at[k, d - 1], y_peer)

    def gather_y(k, d):
        at = G.at[k, z_at(Z - d) * 2 + y]
        return remote(at, at, gy_s.at[k, d], gy_r.at[k, d], y_peer)

    def gather_y_in(k, d):
        at = G.at[k, z_at(Z - d) * 2 + 1 - y]
        return remote(at, at, gy_s.at[k, d], gy_r.at[k, d], y_peer)

    def start_gather(k, carry):
        for d in range(1, Z):
            gather_z(k, d).start()
        gather_y(k, 0).start()
        return carry

    lax.fori_loop(0, AHEAD, start_gather, 0)
    F[...] = jnp.zeros_like(F)
    acc[...] = jnp.zeros_like(acc)

    def forward(k):
        for d in range(1, Z):
            gather_z_in(k, d).wait_recv()
            gather_y(k, d).start()

    forward(0)

    def reduce_core(c):
        return remote(F.at[c, 1 - q], r1.at[c], e1_s.at[c], e1_r.at[c], core_peer)

    def reduce_x(c, d):
        return remote(s2.at[c, d - 1], r2.at[c, d - 1], e2_s.at[c, d - 1], e2_r.at[c, d - 1], (v, x_at(d) * 2 + q))

    def sum_cores(c, carry):
        reduce_core(c).wait_recv()
        for d in range(1, X):
            s2[c, d - 1] = F[c, q, x_at(d)] + r1[c, x_at(d)]
            reduce_x(c, d).start()
        return carry

    def share_x(c, d):
        at = SH.at[c, p]
        return remote(at, at, e3_s.at[c, d - 1], e3_r.at[c, d - 1], (v, x_at(d) * 2 + q))

    def share_x_in(c, d):
        at = SH.at[c, x_at(X - d) * 2 + q]
        return remote(at, at, e3_s.at[c, d - 1], e3_r.at[c, d - 1], core_peer)

    def share_core(c, d):
        at = SH.at[c, x_at(X - d) * 2 + q]
        return remote(at, at, e4_s.at[c, d], e4_r.at[c, d], core_peer)

    def share_core_in(c, d):
        at = SH.at[c, x_at(X - d) * 2 + 1 - q]
        return remote(at, at, e4_s.at[c, d], e4_r.at[c, d], core_peer)

    def shift(c, carry):
        h = c // NC
        total = F[c, q, x] + r1[c, x]
        for d in range(1, X):
            reduce_x(c, d).wait_recv()
            total += r2[c, d - 1]
        bias = jnp.tanh(total)
        cols = pl.ds(pl.multiple_of(c % NC * CB, CB), CB)
        field = fbuf[:, h, :, cols].reshape(S2, CB).astype(jnp.float32)
        SH[c, p] = (field - bias).astype(jnp.bfloat16)
        for d in range(1, X):
            share_x(c, d).start()
        share_core(c, 0).start()
        terms = field * bias - 0.5 * bias * bias
        add = terms[:, :128]
        for j in range(1, CB // 128):
            add += terms[:, j * 128:(j + 1) * 128]
        acc[:VS, h] += add.reshape(VS, HL, 128)
        return carry

    def share_weight(d):
        return remote(lw_in.at[0], lw_in.at[d], lw_s.at[d - 1], lw_r.at[d - 1], (lax.rem(v + d, V), p))

    def pass_core(c, carry):
        for d in range(1, X):
            share_x_in(c, d).wait_recv()
            share_core(c, d).start()
        return carry

    def take_core(c, carry):
        for d in range(X):
            share_core_in(c, d).wait_recv()
        return carry

    def send_weight():
        lw_in[0] = lax.dot_general(
            jnp.ones((8, 128), jnp.float32), acc[...].reshape(128, 128), (((1,), (1,)), ((), ())),
            precision=lax.Precision.HIGHEST, preferred_element_type=jnp.float32,
        )
        for d in range(1, V):
            share_weight(d).start()

    def force_step(i, carry):
        k, c = i // NC, i % NC

        @pl.when(c == 0)
        def _():
            @pl.when(k < 2 * NK - 1)
            def _():
                forward(k + 1)

            @pl.when(k + AHEAD < 2 * NK)
            def _():
                start_gather(k + AHEAD, 0)

            for d in range(Z):
                gather_y_in(k, d).wait_recv()

        @pl.when(i + BUFS - 1 < 2 * NK * NC)
        def _():
            chol1(i + BUFS - 1).start()

        chol1(i).wait()
        part = lax.dot_general(
            G[k].reshape(W2, KB), cb1[i % BUFS], (((1,), (1,)), ((), ())), preferred_element_type=jnp.float32
        ).reshape(X, 2, S2, CB)
        e = k // NK * NC + c
        for h in range(2):
            F[e, h] += part[:, h]

        @pl.when(k % NK == NK - 1)
        def _():
            reduce_core(e).start()

        for at, stage in enumerate((sum_cores, shift, pass_core, take_core)):
            @pl.when(k == NK + at)
            def _():
                stage(c, 0)

        return carry

    load_fields.wait()
    lax.fori_loop(0, 2 * NK * NC, force_step, 0)
    lax.fori_loop(NC, 2 * NC, sum_cores, 0)

    def scatter_y(b):
        return remote(yS.at[b], yR.at[b], py_s.at[b], py_r.at[b], y_peer)

    def scatter_z(b, d):
        return remote(zS.at[b, d - 1], zR.at[b, d - 1], pz_s.at[b, d - 1], pz_r.at[b, d - 1], (z_at(d) * 2 + y, p))

    def potential_step(b, carry):
        @pl.when(b == NB * 3 // 8)
        def _():
            lax.fori_loop(NC, 2 * NC, shift, 0)

        @pl.when(b == NB * 6 // 8)
        def _():
            lax.fori_loop(NC, 2 * NC, pass_core, 0)
            send_weight()

        @pl.when(b == NB)
        def _():
            lax.fori_loop(NC, 2 * NC, take_core, 0)

        @pl.when(b < 2 * NB)
        def _():
            @pl.when(b + 1 < 2 * NB)
            def _():
                chol2(b + 1).start()

            chol2(b).wait()
            slot = b % 2
            total = jnp.zeros((W2, TN), jnp.float32)
            for c in range(NC):
                total += jnp.dot(
                    SH[b // NB * NC + c].reshape(W2, CB), cb2[slot, c * CB:(c + 1) * CB, :],
                    preferred_element_type=jnp.float32,
                )
            tmp[...] = total.reshape(Z, 2, HL, TN)
            yS[b] = tmp[:, 1 - y].astype(jnp.bfloat16)
            scatter_y(b).start()
            keep[b] = tmp[:, y]

        @pl.when(b >= LAG)
        def _():
            e = b - LAG
            scatter_y(e).wait_recv()
            for d in range(1, Z):
                zS[e, d - 1] = (keep[e, z_at(d)] + yR[e, z_at(d)].astype(jnp.float32)).astype(jnp.bfloat16)
                scatter_z(e, d).start()

        return carry

    lax.fori_loop(0, 2 * NB + LAG, potential_step, 0)

    def finish(b, carry):
        total = keep[b, z] + yR[b, z].astype(jnp.float32)
        for d in range(1, Z):
            scatter_z(b, d).wait_recv()
            total += zR[b, d - 1].astype(jnp.float32)
        rows = pl.ds(pl.multiple_of(b // NB * HL, HL), HL)
        out_ref[rows, pl.ds(pl.multiple_of(b % NB * TN, TN), TN)] = total
        return carry

    lax.fori_loop(0, 2 * NB, finish, 0)

    weight = lw_in[0]
    for d in range(1, V):
        share_weight(d).wait_recv()
        weight += lw_in[d]
        share_weight(d).wait_send()
    lw_ref[...] = weight

    def sent_gather(k, carry):
        for d in range(1, Z):
            gather_z(k, d).wait_send()
        for d in range(Z):
            gather_y(k, d).wait_send()
        return carry

    lax.fori_loop(0, 2 * NK, sent_gather, 0)

    def sent_share(c, carry):
        reduce_core(c).wait_send()
        for d in range(1, X):
            reduce_x(c, d).wait_send()
            share_x(c, d).wait_send()
        for d in range(X):
            share_core(c, d).wait_send()
        return carry

    lax.fori_loop(0, 2 * NC, sent_share, 0)

    def sent_scatter(b, carry):
        scatter_y(b).wait_send()
        for d in range(1, Z):
            scatter_z(b, d).wait_send()
        return carry

    lax.fori_loop(0, 2 * NB, sent_scatter, 0)


def shards(green, chol, fields):
    V, NP = lax.axis_size("vec"), lax.axis_size("pair")
    Z, X = V // 2, NP // 2
    LW, K = green.shape
    C = chol.shape[0]
    W = V * LW
    S = W // NP
    HL, S2 = LW // 2, S // 2
    NK = 4
    KB = K // NK
    CB = 512
    NC = C // CB
    TN = 1024
    NB = K // TN
    dims = (V, Z, NP, X, LW, S, C, K, NK, KB, NC, CB, NB, TN)
    bf, f32 = jnp.bfloat16, jnp.float32
    dma = pltpu.SemaphoreType.DMA
    potential, weight = pl.pallas_call(
        functools.partial(kernel, dims),
        out_shape=(jax.ShapeDtypeStruct((LW, K), f32), jax.ShapeDtypeStruct((8, 128), f32)),
        in_specs=[
            pl.BlockSpec(memory_space=pltpu.VMEM),
            pl.BlockSpec(memory_space=pl.ANY),
            pl.BlockSpec(memory_space=pl.ANY),
        ],
        out_specs=(pl.BlockSpec(memory_space=pltpu.VMEM), pl.BlockSpec(memory_space=pltpu.VMEM)),
        scratch_shapes=[
            pltpu.VMEM((2 * NK, V, HL, KB), bf),
            pltpu.VMEM((2 * NC, 2, X, S2, CB), f32),
            pltpu.VMEM((2 * NC, X, S2, CB), f32),
            pltpu.VMEM((2 * NC, X - 1, S2, CB), f32),
            pltpu.VMEM((2 * NC, X - 1, S2, CB), f32),
            pltpu.VMEM((2 * NC, NP, S2, CB), bf),
            pltpu.VMEM((S // LW, 2, HL, C), bf),
            pltpu.VMEM((128 // LW, 2, HL, 128), f32),
            pltpu.VMEM((BUFS, CB, KB), bf),
            pltpu.VMEM((2, C, TN), bf),
            pltpu.VMEM((Z, 2, HL, TN), f32),
            pltpu.VMEM((2 * NB, Z, HL, TN), bf),
            pltpu.VMEM((2 * NB, Z, HL, TN), bf),
            pltpu.VMEM((2 * NB, Z, HL, TN), f32),
            pltpu.VMEM((2 * NB, Z - 1, HL, TN), bf),
            pltpu.VMEM((2 * NB, Z - 1, HL, TN), bf),
            pltpu.VMEM((V, 8, 128), f32),
            dma((BUFS,)), dma((2,)), dma(()),
            dma((2 * NK, Z - 1)), dma((2 * NK, Z - 1)), dma((2 * NK, Z)), dma((2 * NK, Z)),
            dma((2 * NC,)), dma((2 * NC,)), dma((2 * NC, X - 1)), dma((2 * NC, X - 1)),
            dma((2 * NC, X - 1)), dma((2 * NC, X - 1)), dma((2 * NC, X)), dma((2 * NC, X)),
            dma((2 * NB,)), dma((2 * NB,)), dma((2 * NB, Z - 1)), dma((2 * NB, Z - 1)),
            dma((V - 1,)), dma((V - 1,)),
        ],
        compiler_params=pltpu.CompilerParams(
            collective_id=0, has_side_effects=True, vmem_limit_bytes=56 * 1024 * 1024
        ),
        name="walker_step",
    )(green, chol, fields.reshape(V, 2, HL, C))
    return potential, weight[0, :S] / (C * V)


def solution(mesh):
    return jax.shard_map(
        shards,
        mesh=mesh,
        in_specs=(P("vec", "pair"), P("vec", "pair"), P(None, "vec")),
        out_specs=(P("vec", "pair"), P("pair")),
        check_vma=False,
    )
```
